32 devices in a mesh: groups: 2 (over y), patch: 4 (over z), req: 4 (over x, core).
Axes of the slice: x: 2, y: 2, z: 4, core: 2. Of those that a mesh axis runs over, the one named last changes fastest.
Arguments:
- hidden: bfloat16 [2, 8, 2, 128, 1152], P(None, ('groups', 'req'), None, 'patch'), parts along dimension 1, may hold values from -6 to 6
- stale_kv: bfloat16 [8, 2, 128, 1152], P(('groups', 'req'), None, 'patch'), parts along dimension 0
- cond_kv: bfloat16 [8, 128, 1152], P(('groups', 'req')), parts along dimension 0
- uncond_kv: bfloat16 [128, 1152], P('req')
- text_len: int32 [8], P(('groups', 'req')), parts along dimension 0, may hold values from 1 to 128, as said below
- timestep: int32 [8, 2], P(('groups', 'req')), parts along dimension 0, may hold values from 0 to 19
- mod_table: float32 [20, 3, 1152], replicated, may hold values from -4 to 4
- w_qkv: bfloat16 [1152, 1728], P('req'), may hold values from -0.26953125 to 0.26953125
- w_out: bfloat16 [576, 1152], P('req'), may hold values from -0.25 to 0.25
- w_cq: bfloat16 [1152, 576], P('req'), may hold values from -0.26953125 to 0.26953125
- w_co: bfloat16 [576, 1152], P('req'), may hold values from -0.25 to 0.25
Outputs:
- mixed: bfloat16 [2, 8, 2, 128, 1152], P(None, ('groups', 'req'), None, 'patch'), parts along dimension 1
- next_kv: bfloat16 [8, 2, 128, 1152], P(('groups', 'req'), None, 'patch'), parts along dimension 0
The draws below stay inside these ranges and needn't reach their ends.
There are 2 independent parts, one for each index of `groups`. The reference program is written for one: setup_inputs(seed, part) draws one part's arguments, and reference() takes and returns one part's arrays. A program takes and returns all parts, laid end to end along the dimension named above; an argument that names none is the same for every part. Nothing has to cross between parts.
Inputs may be any that keep to these rules, and one draw needn't show every extreme that they name: `text_len`: some request's prompt has all 128 tokens.
All inputs are finite; a program needn't handle non-finite values.
Results may differ from the reference program's by a relative error of at most 0.02.
Values may be sent and summed in bfloat16 or wider, within the bound.
A program may use at most 128 MiB of HBM per device.

```python
import math
import jax
import jax.numpy as jnp
from jax import lax

D = 1152
HEADS = 8
HDIM = 72
TOK_DEV = 32
TEXT = 128
TSTEPS = 20
INNER = 576
TOKENS = 128
REQS = 4
N_PATCH = 4


def pair_rows(key, lead, rows):
    shape = lead + (rows, 2 * INNER)
    first = jax.random.fold_in(key, 0)
    base = jax.random.normal(first, shape, jnp.float32)
    key_scale = 1.5
    is_key = jnp.arange(2 * INNER) < INNER
    return (base * jnp.where(is_key, key_scale, 1.0)).astype(jnp.bfloat16)


def draw_stale_kv(key, part):
    return pair_rows(jax.random.fold_in(key, 11), (REQS, 2), TOKENS)


def draw_cond_kv(key, part):
    return pair_rows(jax.random.fold_in(key, 23), (REQS,), TEXT)


def draw_uncond_kv(key, part):
    return pair_rows(jax.random.fold_in(key, 37), (), TEXT)


def draw_text_len(key, part):
    first, second = jax.random.split(jax.random.fold_in(key, 51))
    lengths = jax.random.randint(first, (REQS,), 1, TEXT + 1)
    chosen = jax.random.randint(second, (), 0, REQS)
    return lengths.at[chosen].set(TEXT).astype(jnp.int32)


def place_ends(values, rng, low, high):
    longest = values.shape.index(max(values.shape))
    spots = []
    for shift in (0, 1):
        where = [jax.random.randint(jax.random.fold_in(rng, axis), (), 0, length) for axis, length in enumerate(values.shape)]
        where[longest] = (where[longest] + shift) % values.shape[longest]
        spots.append(tuple(where))
    return values.at[spots[0]].set(low).at[spots[1]].set(high)


def block_scale(own_key, shape, shards, low, top_value):
    gain = 1.0
    for dim, blocks in shards:
        heights = jax.random.uniform(jax.random.fold_in(jax.random.fold_in(own_key, 6), dim), (blocks,), jnp.float32, low / len(shards), top_value / len(shards))
        gain = gain * jnp.repeat(jnp.exp(heights), shape[dim] // blocks).reshape((-1,) + (1,) * (len(shape) - 1 - dim))
    return gain


def centred(stream_key, dims, deviation, bound, shards=(), kind=jnp.bfloat16):
    entries = deviation * jax.random.normal(stream_key, dims, jnp.float32)
    if shards:
        entries = entries * block_scale(stream_key, dims, shards, -0.22, 0.18)
    return jnp.clip(entries, -bound, bound).astype(kind)


def setup_inputs(seed: int = 0, part: int = 0) -> dict:
    key_of = jax.random.split(jax.random.key(seed), 12)
    part_splits = jax.random.split(jax.random.fold_in(key_of[11], part), 12)
    return {
        "hidden": centred(part_splits[0], (2, REQS, 2, TOKENS, D), 1.0, 6.0, ((1, 4), (3, 4))),
        "stale_kv": draw_stale_kv(jax.random.fold_in(jax.random.fold_in(key_of[11], part), 71), part),
        "cond_kv": draw_cond_kv(jax.random.fold_in(jax.random.fold_in(key_of[11], part), 71), part),
        "uncond_kv": draw_uncond_kv(jax.random.fold_in(key_of[11], 71), part),
        "text_len": draw_text_len(jax.random.fold_in(jax.random.fold_in(key_of[11], part), 71), part),
        "timestep": place_ends(jax.random.randint(part_splits[5], (REQS, 2), 0, TSTEPS), jax.random.fold_in(part_splits[5], 1), 0, TSTEPS - 1).astype(jnp.int32),
        "mod_table": centred(key_of[6], (TSTEPS, 3, D), 0.8, 4.0, (), jnp.float32),
        "w_qkv": centred(key_of[7], (D, 3 * INNER), 0.045, 0.26953125, ((0, 4),)),
        "w_out": centred(key_of[8], (INNER, D), INNER ** -0.5, 0.25, ((0, 4),)),
        "w_cq": centred(key_of[9], (D, INNER), 0.045, 0.26953125, ((0, 4),)),
        "w_co": centred(key_of[10], (INNER, D), INNER ** -0.5, 0.25, ((0, 4),)),
    }


def layer_norm(values):
    center = values - lax.optimization_barrier(jnp.mean(values, axis=-1, keepdims=True))
    spread = lax.optimization_barrier(jnp.mean(center * center, axis=-1, keepdims=True))
    return center * lax.rsqrt(spread + 1e-06)

def attend(query, pairs, mask):
    batch, count, inner = query.shape
    keys_n = pairs.shape[1]
    factor = 1.0 / math.sqrt(HDIM)
    q_heads = query.reshape(batch, count, HEADS, HDIM).astype(jnp.float32)
    k_heads = pairs[:, :, :inner].reshape(batch, keys_n, HEADS, HDIM).astype(jnp.float32)
    v_heads = pairs[:, :, inner:].reshape(batch, keys_n, HEADS, HDIM).astype(jnp.float32)
    scores = jnp.einsum('bqhd,bkhd->bhqk', q_heads, k_heads) * factor
    if mask is not None:
        scores = jnp.where(mask[:, None, None, :], scores, -1e+30)
    peak = lax.optimization_barrier(jnp.max(scores, axis=-1, keepdims=True))
    expo = jnp.exp(scores - peak)
    total = lax.optimization_barrier(jnp.sum(expo, axis=-1))
    weights = expo.astype(jnp.bfloat16).astype(jnp.float32)
    summed = jnp.einsum('bhqk,bkhd->bqhd', weights, v_heads)
    result = summed / jnp.transpose(total, (0, 2, 1))[..., None]
    return result.reshape(batch, count, inner).astype(jnp.bfloat16)

def self_attend(query, earlier, fresh):

    def one_block(block):
        start = (block * TOK_DEV).astype(jnp.int32)
        q_block = lax.dynamic_slice_in_dim(query, start, TOK_DEV, 1)
        f_block = lax.dynamic_slice_in_dim(fresh, start, TOK_DEV, 1)
        pairs = lax.dynamic_update_slice_in_dim(earlier, f_block, start, 1)
        return attend(q_block, pairs, None)
    blocks = lax.map(one_block, jnp.arange(N_PATCH, dtype=jnp.int32))
    batch = query.shape[0]
    return jnp.transpose(blocks, (1, 0, 2, 3)).reshape(batch, TOKENS, INNER)

def reference(hidden, stale_kv, cond_kv, uncond_kv, text_len, timestep, mod_table, w_qkv, w_out, w_cq, w_co):
    mods = mod_table[timestep]
    text_mask = jnp.arange(TEXT, dtype=jnp.int32)[None, :] < text_len[:, None]
    negative = jnp.broadcast_to(uncond_kv[None], (REQS, TEXT, 2 * INNER))
    earlier = stale_kv.reshape(REQS * 2, TOKENS, 2 * INNER)
    results = []
    fresh = earlier
    for step in range(2):
        shift = mods[:, step, 0][:, None, None, :]
        scale = mods[:, step, 1][:, None, None, :]
        gate = mods[:, step, 2][:, None, None, :]
        source = hidden[step].astype(jnp.float32)
        modulated = (layer_norm(source) * (1.0 + scale) + shift).astype(jnp.bfloat16)
        qkv = jnp.dot(modulated.reshape(-1, D), w_qkv, preferred_element_type=jnp.float32).astype(jnp.bfloat16)
        qkv = qkv.reshape(REQS * 2, TOKENS, 3 * INNER)
        query = qkv[:, :, :INNER]
        fresh = qkv[:, :, INNER:]
        attended = self_attend(query, earlier, fresh)
        projected = jnp.dot(attended.reshape(-1, INNER), w_out, preferred_element_type=jnp.float32)
        x_one = (source + gate * projected.reshape(REQS, 2, TOKENS, D)).astype(jnp.bfloat16)
        cross_query = jnp.dot(x_one.reshape(-1, D), w_cq, preferred_element_type=jnp.float32).astype(jnp.bfloat16)
        cross_query = cross_query.reshape(REQS, 2, TOKENS, INNER)
        cond_out = attend(cross_query[:, 0], cond_kv, text_mask)
        uncond_out = attend(cross_query[:, 1], negative, None)
        cross = jnp.stack([cond_out, uncond_out], axis=1)
        added = jnp.dot(cross.reshape(-1, INNER), w_co, preferred_element_type=jnp.float32)
        mixed = (x_one.astype(jnp.float32) + added.reshape(REQS, 2, TOKENS, D)).astype(jnp.bfloat16)
        results.append(mixed)
        earlier = fresh
    next_kv = fresh.reshape(REQS, 2, TOKENS, 2 * INNER)
    return (jnp.stack(results, axis=0), next_kv)
```

```python
import functools
import math

import jax
import jax.numpy as jnp
from jax import lax
from jax.experimental import pallas as pl
from jax.experimental.pallas import tpu as pltpu
from jax.sharding import PartitionSpec as P

HEADS = 8
HDIM = 72
CORES = 2
LANES = 128
MESH = pl.DeviceIdType.MESH

QKV, OUT, CQ, CO, NEG = range(5)


def spread(which, start, stop, groups):
    width = (stop - start) // (LANES * groups) * LANES
    chunks = []
    if width:
        chunks.append((which, start, width, True))
    if stop > start + groups * width:
        chunks.append((which, start + groups * width, stop - start - groups * width, False))
    return chunks


def plan(inner, width, groups):
    low = inner // LANES * LANES
    first = spread(QKV, low, 3 * inner, groups)
    stages = [
        first,
        spread(QKV, 0, low, groups),
        spread(OUT, 0, width, groups),
        spread(CQ, 0, inner, groups) + spread(NEG, 0, 2 * inner, groups),
        spread(CO, 0, width, groups),
    ]
    return stages


def times(left, w_ref):
    n, rows, _ = w_ref.shape
    if rows % 16 == 0:
        return jnp.dot(
            left,
            w_ref[...].reshape(n * rows, w_ref.shape[2]),
            preferred_element_type=jnp.float32,
        )
    total = None
    for s in range(n):
        term = jnp.dot(
            left[:, s * rows : (s + 1) * rows], w_ref[s], preferred_element_type=jnp.float32
        )
        total = term if total is None else total + term
    return total


def head_mask(lanes, offset, dtype):
    lane = lax.broadcasted_iota(jnp.int32, (HEADS, 1, lanes), 2) - offset
    first = lax.broadcasted_iota(jnp.int32, (HEADS, 1, lanes), 0) * HDIM
    return jnp.where((lane >= first) & (lane < first + HDIM), 1.0, 0.0).astype(dtype)


def attend(query, keys, values, q_mask, v_mask, count):
    rows, inner = query.shape
    stacked = (query[None] * q_mask).reshape(HEADS * rows, inner)
    scores = lax.dot_general(
        stacked, keys, (((1,), (1,)), ((), ())), preferred_element_type=jnp.float32
    ) * (1.0 / math.sqrt(HDIM))
    if count is not None:
        place = lax.broadcasted_iota(jnp.int32, scores.shape, 1)
        scores = jnp.where(place < count, scores, -1e30)
    expo = jnp.exp(scores - jnp.max(scores, axis=-1, keepdims=True))
    total = jnp.sum(expo, axis=-1, keepdims=True)
    summed = jnp.dot(expo.astype(jnp.bfloat16), values, preferred_element_type=jnp.float32)
    scaled = (summed * (1.0 / total)).reshape(HEADS, rows, values.shape[1])
    return jnp.sum(scaled * v_mask, axis=0)


def kernel(
    groups, patch_n, req_n, stages,
    len_ref, step_ref, hidden_ref, stale_ref, cond_ref, neg_in, table_ref, qkv_in, out_in, cq_in, co_in,
    mixed_ref, next_ref,
    w_qkv, w_out, w_cq, w_co, w_neg, kv0, kv1, mod_s, query_s, att_s,
    local_sem, own_send, own_recv, x_send, x_recv, y_send, y_recv, fx_send, fx_recv, fy_send, fy_recv,
    s_send, s_recv, f_send, f_recv,
):
    chips = req_n // CORES
    group = lax.axis_index("groups")
    patch = lax.axis_index("patch")
    req = lax.axis_index("req")
    chip, core = req // CORES, req % CORES
    sibling = (group, patch, chip * CORES + (1 - core))
    sources = (qkv_in, out_in, cq_in, co_in, neg_in)
    bufs = (w_qkv, w_out, w_cq, w_co, w_neg)
    inner = cq_in.shape[1]
    low = inner // LANES * LANES
    high = low + LANES if low < inner else low

    def chip_at(delta):
        return lax.rem(chip + (delta + chips), chips) * CORES + core

    def group_at(delta):
        return lax.rem(group + (delta + groups), groups)

    def patch_at(delta):
        return lax.rem(patch + (delta + patch_n), patch_n)

    barrier = pltpu.get_barrier_semaphore()
    friends = [sibling]
    friends += [(group, patch, chip_at(d)) for d in range(1, chips)]
    friends += [(group_at(e), patch, req) for e in range(1, groups)]
    friends += [(group, patch_at(d), req) for d in range(1, patch_n)]
    for friend in friends:
        pl.semaphore_signal(barrier, inc=1, device_id=friend, device_id_type=MESH)
    pl.semaphore_wait(barrier, len(friends))

    chunks = [chunk for stage in stages for chunk in stage]

    def columns(chunk, owner):
        _, start, width, shared = chunk
        if not shared:
            return pl.ds(start, width)
        return pl.ds(pl.multiple_of(start + owner * width, LANES), width)

    def remote(src, dst, send, recv, target):
        return pltpu.make_async_remote_copy(
            src_ref=src, dst_ref=dst, send_sem=send, recv_sem=recv,
            device_id=target, device_id_type=MESH,
        )

    def x_copy(k, d):
        chunk = chunks[k]
        cols = columns(chunk, group)
        return remote(
            sources[chunk[0]].at[:, cols], bufs[chunk[0]].at[req, :, cols],
            x_send.at[k, d - 1], x_recv.at[k, d - 1], (group, patch, chip_at(d)),
        )

    def arrived(k, d, owner, send, recv, target):
        part = bufs[chunks[k][0]].at[chip_at(-d), :, columns(chunks[k], owner)]
        return remote(part, part, send, recv, target)

    def x_arrival(k, d):
        return arrived(k, d, group, x_send.at[k, d - 1], x_recv.at[k, d - 1], sibling)

    def y_copy(k, d, e):
        return arrived(
            k, d, group, y_send.at[k, d - 1, e - 1], y_recv.at[k, d - 1, e - 1],
            (group_at(e), patch, req),
        )

    def y_arrival(k, d, e):
        return arrived(
            k, d, group_at(-e), y_send.at[k, d - 1, e - 1], y_recv.at[k, d - 1, e - 1], sibling
        )

    def fx_copy(k, d):
        return arrived(k, d, group, fx_send.at[k, d - 1], fx_recv.at[k, d - 1], sibling)

    def fy_copy(k, d, e):
        return arrived(
            k, d, group_at(-e), fy_send.at[k, d - 1, e - 1], fy_recv.at[k, d - 1, e - 1], sibling
        )

    def other_core(k, d, owner, send, recv):
        source = lax.rem(chip + (chips - d), chips) * CORES + (1 - core)
        part = bufs[chunks[k][0]].at[source, :, columns(chunks[k], owner)]
        return remote(part, part, send, recv, sibling)

    def own_copy(i, slot):
        return remote(
            sources[i], bufs[i].at[slot], own_send.at[i], own_recv.at[i], sibling
        )

    def keep(i):
        return pltpu.make_async_copy(sources[i], bufs[i].at[req], local_sem.at[i])

    def stale_copy(d, slot):
        return remote(
            stale_ref, kv0.at[slot], s_send.at[d - 1], s_recv.at[d - 1],
            (group, patch_at(d), req),
        )

    def fresh_copy(d, slot):
        return remote(
            kv0.at[patch], kv1.at[slot], f_send.at[d - 1], f_recv.at[d - 1],
            (group, patch_at(d), req),
        )

    index = {}
    place = 0
    for number, stage in enumerate(stages):
        index[number] = list(range(place, place + len(stage)))
        place += len(stage)

    for k in range(len(chunks)):
        for d in range(1, chips):
            x_copy(k, d).start()
    for i in range(len(sources)):
        keep(i).start()
        own_copy(i, req).start()
    for d in range(1, patch_n):
        stale_copy(d, patch).start()

    def relay(number):
        for k in index[number]:
            for d in range(1, chips):
                x_arrival(k, d).wait_recv()
                if chunks[k][3]:
                    for e in range(1, groups):
                        y_copy(k, d, e).start()
                fx_copy(k, d).start()

    def relay_two(number):
        for k in index[number]:
            if chunks[k][3]:
                for d in range(1, chips):
                    for e in range(1, groups):
                        y_arrival(k, d, e).wait_recv()
                        fy_copy(k, d, e).start()

    def land(number):
        for k in index[number]:
            for d in range(1, chips):
                other_core(k, d, group, fx_send.at[k, d - 1], fx_recv.at[k, d - 1]).wait_recv()
                if chunks[k][3]:
                    for e in range(1, groups):
                        other_core(
                            k, d, group_at(-e),
                            fy_send.at[k, d - 1, e - 1], fy_recv.at[k, d - 1, e - 1],
                        ).wait_recv()

    def own_land(i):
        keep(i).wait()
        own_copy(i, chip * CORES + (1 - core)).wait_recv()

    rows = hidden_ref.shape[0] // 2
    images = 2
    tok = rows // images
    width = hidden_ref.shape[1]
    mods = [table_ref[step_ref[0, s]] for s in range(2)]
    for s in range(2):
        source = hidden_ref[s * rows : (s + 1) * rows, :].astype(jnp.float32)
        center = source - jnp.mean(source, axis=-1, keepdims=True)
        spread_ = jnp.mean(center * center, axis=-1, keepdims=True)
        normed = center * lax.rsqrt(spread_ + 1e-06)
        mod_s[s * rows : (s + 1) * rows, :] = (
            normed * (1.0 + mods[s][1:2]) + mods[s][0:1]
        ).astype(jnp.bfloat16)

    def project(first, last, start, stop):
        n, depth, _ = w_qkv.shape
        return jnp.dot(
            mod_s[first:last, :], w_qkv[:, :, start:stop].reshape(n * depth, stop - start),
            preferred_element_type=jnp.float32,
        ).astype(jnp.bfloat16)

    relay(0)
    relay_two(0)
    own_land(QKV)
    land(0)
    fresh0 = project(0, rows, low, 3 * inner)[:, inner - low :]
    kv0[patch] = fresh0.reshape(images, tok, 2 * inner)
    for d in range(1, patch_n):
        fresh_copy(d, patch).start()
    relay(1)
    fresh1 = project(rows, 2 * rows, low, 3 * inner)[:, inner - low :]
    kv1[patch] = fresh1.reshape(images, tok, 2 * inner)
    next_ref[...] = fresh1
    relay_two(1)
    land(1)
    query_s[...] = project(0, 2 * rows, 0, high)[:, :inner]
    relay(2)

    q_mask = head_mask(inner, 0, jnp.bfloat16)
    v_mask = head_mask(2 * inner - low, inner - low, jnp.float32)

    def self_attend(step, buf):
        for image in range(images):
            first = step * rows + image * tok
            pairs = buf[:, image].reshape(patch_n * tok, 2 * inner)
            result = attend(
                query_s[first : first + tok, :], pairs[:, :inner], pairs[:, low:],
                q_mask, v_mask, None,
            )
            att_s[first : first + tok, :] = result[:, inner - low :].astype(jnp.bfloat16)

    for d in range(1, patch_n):
        stale_copy(d, patch_at(-d)).wait_recv()
    self_attend(0, kv0)
    relay_two(2)
    relay(3)
    relay_two(3)
    relay(4)
    for d in range(1, patch_n):
        fresh_copy(d, patch_at(-d)).wait_recv()
    self_attend(1, kv1)
    relay_two(4)
    own_land(OUT)
    land(2)
    projected = times(att_s[...], w_out)
    parts = []
    for s in range(2):
        span = slice(s * rows, (s + 1) * rows)
        parts.append(
            (hidden_ref[span, :].astype(jnp.float32) + mods[s][2:3] * projected[span]).astype(
                jnp.bfloat16
            )
        )
    x_one = jnp.concatenate(parts, axis=0)
    own_land(CQ)
    own_land(NEG)
    land(3)
    cross_query = times(x_one, w_cq).astype(jnp.bfloat16)
    count = len_ref[0]
    n_neg, neg_rows, _ = w_neg.shape
    negative = w_neg[...].reshape(n_neg * neg_rows, 2 * inner)
    for image in range(images):
        pairs = cond_ref[...] if image == 0 else negative
        spans = [slice(s * rows + image * tok, s * rows + (image + 1) * tok) for s in range(2)]
        both = jnp.concatenate([cross_query[span] for span in spans], axis=0)
        result = attend(
            both, pairs[:, :inner], pairs[:, low:], q_mask, v_mask, count if image == 0 else None
        )[:, inner - low :].astype(jnp.bfloat16)
        for s in range(2):
            att_s[spans[s], :] = result[s * tok : (s + 1) * tok]
    own_land(CO)
    land(4)
    added = times(att_s[...], w_co)
    mixed_ref[...] = (x_one.astype(jnp.float32) + added).astype(jnp.bfloat16)

    for k in range(len(chunks)):
        for d in range(1, chips):
            x_copy(k, d).wait_send()
            fx_copy(k, d).wait_send()
            if chunks[k][3]:
                for e in range(1, groups):
                    y_copy(k, d, e).wait_send()
                    fy_copy(k, d, e).wait_send()
    for i in range(len(sources)):
        own_copy(i, req).wait_send()
    for d in range(1, patch_n):
        stale_copy(d, patch).wait_send()
        fresh_copy(d, patch).wait_send()


def solution(mesh):
    groups, patch_n, req_n = mesh.shape["groups"], mesh.shape["patch"], mesh.shape["req"]
    chips = req_n // CORES

    def per_device(
        hidden, stale_kv, cond_kv, uncond_kv, text_len, timestep, mod_table, w_qkv, w_out, w_cq, w_co
    ):
        steps_n, req_here, pair_n, tok, width = hidden.shape
        inner = w_cq.shape[1]
        stages = plan(inner, width, groups)
        count = sum(len(stage) for stage in stages)
        total = steps_n * req_here * pair_n * tok
        vmem = pl.BlockSpec(memory_space=pltpu.VMEM)
        anywhere = pl.BlockSpec(memory_space=pl.ANY)
        smem = pl.BlockSpec(memory_space=pltpu.SMEM)
        weights = (w_qkv, w_out, w_cq, w_co, uncond_kv)
        dma = pltpu.SemaphoreType.DMA
        near = (count, max(chips - 1, 1))
        far = near + (max(groups - 1, 1),)
        line = (max(patch_n - 1, 1),)
        mixed, next_kv = pl.pallas_call(
            functools.partial(kernel, groups, patch_n, req_n, stages),
            out_shape=(
                jax.ShapeDtypeStruct((total, width), jnp.bfloat16),
                jax.ShapeDtypeStruct((pair_n * tok, 2 * inner), jnp.bfloat16),
            ),
            in_specs=[
                smem, smem, vmem, anywhere, vmem, anywhere, vmem,
                anywhere, anywhere, anywhere, anywhere,
            ],
            out_specs=(vmem, vmem),
            scratch_shapes=[pltpu.VMEM((req_n,) + w.shape, jnp.bfloat16) for w in weights]
            + [
                pltpu.VMEM((patch_n, pair_n, tok, 2 * inner), jnp.bfloat16),
                pltpu.VMEM((patch_n, pair_n, tok, 2 * inner), jnp.bfloat16),
                pltpu.VMEM((total, width), jnp.bfloat16),
                pltpu.VMEM((total, inner), jnp.bfloat16),
                pltpu.VMEM((total, inner), jnp.bfloat16),
                dma((5,)), dma((5,)), dma((5,)),
                dma(near), dma(near), dma(far), dma(far), dma(near), dma(near), dma(far), dma(far),
                dma(line), dma(line), dma(line), dma(line),
            ],
            compiler_params=pltpu.CompilerParams(
                collective_id=0, has_side_effects=True, vmem_limit_bytes=48 * 1024 * 1024
            ),
        )(
            text_len, timestep, hidden.reshape(total, width),
            stale_kv.reshape(pair_n, tok, 2 * inner), cond_kv.reshape(cond_kv.shape[1:]),
            uncond_kv, mod_table, w_qkv, w_out, w_cq, w_co,
        )
        return mixed.reshape(hidden.shape), next_kv.reshape(stale_kv.shape)

    placed = (
        P(None, ("groups", "req"), None, "patch", None),
        P(("groups", "req"), None, "patch", None),
        P(("groups", "req"), None, None),
        P("req", None),
        P(("groups", "req")),
        P(("groups", "req"), None),
        P(),
        P("req", None),
        P("req", None),
        P("req", None),
        P("req", None),
    )
    return jax.shard_map(
        per_device,
        mesh=mesh,
        in_specs=placed,
        out_specs=(
            P(None, ("groups", "req"), None, "patch", None),
            P(("groups", "req"), None, "patch", None),
        ),
        check_vma=False,
    )
```

```python
import functools
import math

import jax
import jax.numpy as jnp
from jax import lax
from jax.experimental import pallas as pl
from jax.experimental.pallas import tpu as pltpu
from jax.sharding import PartitionSpec as P

HEADS = 8
HDIM = 72
CORES = 2
LANES = 128
PIECE = 256
AHEAD = 3
MESH = pl.DeviceIdType.MESH

QKV, OUT, CQ, CO, NEG = range(5)


def spread(which, start, stop, groups):
    width = (stop - start) // (LANES * groups) * LANES
    chunks = []
    place = start
    while place < start + groups * width:
        piece = min(PIECE, (start + groups * width - place) // groups)
        chunks.append((which, place, piece, True))
        place += groups * piece
    if stop > start + groups * width:
        chunks.append((which, start + groups * width, stop - start - groups * width, False))
    return chunks


def plan(inner, width, groups):
    low = inner // LANES * LANES
    first = spread(QKV, low, 3 * inner, groups)
    stages = [
        first,
        spread(QKV, 0, low, groups),
        spread(OUT, 0, width, groups),
        spread(CQ, 0, inner, groups) + spread(NEG, 0, 2 * inner, groups),
        spread(CO, 0, width, groups),
    ]
    return stages


def times(left, w_ref):
    n, rows, _ = w_ref.shape
    if rows % 16 == 0:
        return jnp.dot(
            left,
            w_ref[...].reshape(n * rows, w_ref.shape[2]),
            preferred_element_type=jnp.float32,
        )
    total = None
    for s in range(n):
        term = jnp.dot(
            left[:, s * rows : (s + 1) * rows], w_ref[s], preferred_element_type=jnp.float32
        )
        total = term if total is None else total + term
    return total


def head_mask(lanes, offset, dtype):
    lane = lax.broadcasted_iota(jnp.int32, (HEADS, 1, lanes), 2) - offset
    first = lax.broadcasted_iota(jnp.int32, (HEADS, 1, lanes), 0) * HDIM
    return jnp.where((lane >= first) & (lane < first + HDIM), 1.0, 0.0).astype(dtype)


def attend(query, keys, values, q_mask, v_mask, count):
    rows, inner = query.shape
    stacked = (query[None] * q_mask).reshape(HEADS * rows, inner)
    scores = lax.dot_general(
        stacked, keys, (((1,), (1,)), ((), ())), preferred_element_type=jnp.float32
    ) * (1.0 / math.sqrt(HDIM))
    if count is not None:
        place = lax.broadcasted_iota(jnp.int32, scores.shape, 1)
        scores = jnp.where(place < count, scores, -1e30)
    expo = jnp.exp(scores - jnp.max(scores, axis=-1, keepdims=True))
    total = jnp.sum(expo, axis=-1, keepdims=True)
    summed = jnp.dot(expo.astype(jnp.bfloat16), values, preferred_element_type=jnp.float32)
    scaled = (summed * (1.0 / total)).reshape(HEADS, rows, values.shape[1])
    return jnp.sum(scaled * v_mask, axis=0)


def kernel(
    groups, patch_n, req_n, stages,
    len_ref, step_ref, hidden_in, stale_ref, cond_in, neg_in, table_in, qkv_in, out_in, cq_in, co_in,
    mixed_ref, next_ref,
    w_qkv, w_out, w_cq, w_co, w_neg, kv0, kv1, mod_s, query_s, att_s,
    hidden_ref, cond_ref, table_ref, in_sem, local_sem, own_send, own_recv, x_send, x_recv, y_send, y_recv, fx_send, fx_recv, fy_send, fy_recv,
    s_send, s_recv, f_send, f_recv,
):
    chips = req_n // CORES
    group = lax.axis_index("groups")
    patch = lax.axis_index("patch")
    req = lax.axis_index("req")
    chip, core = req // CORES, req % CORES
    sibling = (group, patch, chip * CORES + (1 - core))
    sources = (qkv_in, out_in, cq_in, co_in, neg_in)
    bufs = (w_qkv, w_out, w_cq, w_co, w_neg)
    inner = cq_in.shape[1]
    low = inner // LANES * LANES
    high = low + LANES if low < inner else low

    def chip_at(delta):
        return lax.rem(chip + (delta + chips), chips) * CORES + core

    def group_at(delta):
        return lax.rem(group + (delta + groups), groups)

    def patch_at(delta):
        return lax.rem(patch + (delta + patch_n), patch_n)

    staged = [
        pltpu.make_async_copy(src, dst, in_sem.at[i])
        for i, (src, dst) in enumerate(
            ((hidden_in, hidden_ref), (table_in, table_ref), (cond_in, cond_ref))
        )
    ]
    for copy in staged:
        copy.start()
    barrier = pltpu.get_barrier_semaphore()
    friends = [sibling]
    friends += [(group, patch, chip_at(d)) for d in range(1, chips)]
    friends += [(group_at(e), patch, req) for e in range(1, groups)]
    friends += [(group, patch_at(d), req) for d in range(1, patch_n)]
    for friend in friends:
        pl.semaphore_signal(barrier, inc=1, device_id=friend, device_id_type=MESH)
    pl.semaphore_wait(barrier, len(friends))

    chunks = [chunk for stage in stages for chunk in stage]

    def columns(chunk, owner):
        _, start, width, shared = chunk
        if not shared:
            return pl.ds(start, width)
        return pl.ds(pl.multiple_of(start + owner * width, LANES), width)

    def remote(src, dst, send, recv, target):
        return pltpu.make_async_remote_copy(
            src_ref=src, dst_ref=dst, send_sem=send, recv_sem=recv,
            device_id=target, device_id_type=MESH,
        )

    def x_copy(k, d):
        chunk = chunks[k]
        cols = columns(chunk, group)
        return remote(
            sources[chunk[0]].at[:, cols], bufs[chunk[0]].at[req, :, cols],
            x_send.at[k, d - 1], x_recv.at[k, d - 1], (group, patch, chip_at(d)),
        )

    def arrived(k, d, owner, send, recv, target):
        part = bufs[chunks[k][0]].at[chip_at(-d), :, columns(chunks[k], owner)]
        return remote(part, part, send, recv, target)

    def x_arrival(k, d):
        return arrived(k, d, group, x_send.at[k, d - 1], x_recv.at[k, d - 1], sibling)

    def y_copy(k, d, e):
        return arrived(
            k, d, group, y_send.at[k, d - 1, e - 1], y_recv.at[k, d - 1, e - 1],
            (group_at(e), patch, req),
        )

    def y_arrival(k, d, e):
        return arrived(
            k, d, group_at(-e), y_send.at[k, d - 1, e - 1], y_recv.at[k, d - 1, e - 1], sibling
        )

    def fx_copy(k, d):
        return arrived(k, d, group, fx_send.at[k, d - 1], fx_recv.at[k, d - 1], sibling)

    def fy_copy(k, d, e):
        return arrived(
            k, d, group_at(-e), fy_send.at[k, d - 1, e - 1], fy_recv.at[k, d - 1, e - 1], sibling
        )

    def other_core(k, d, owner, send, recv):
        source = lax.rem(chip + (chips - d), chips) * CORES + (1 - core)
        part = bufs[chunks[k][0]].at[source, :, columns(chunks[k], owner)]
        return remote(part, part, send, recv, sibling)

    def own_copy(i, slot):
        return remote(
            sources[i], bufs[i].at[slot], own_send.at[i], own_recv.at[i], sibling
        )

    def keep(i):
        return pltpu.make_async_copy(sources[i], bufs[i].at[req], local_sem.at[i])

    def stale_copy(d, slot):
        return remote(
            stale_ref, kv0.at[slot], s_send.at[d - 1], s_recv.at[d - 1],
            (group, patch_at(d), req),
        )

    def fresh_copy(d, slot):
        return remote(
            kv0.at[patch], kv1.at[slot], f_send.at[d - 1], f_recv.at[d - 1],
            (group, patch_at(d), req),
        )

    index = {}
    place = 0
    for number, stage in enumerate(stages):
        index[number] = list(range(place, place + len(stage)))
        place += len(stage)

    for k in range(min(AHEAD, len(chunks))):
        for d in range(1, chips):
            x_copy(k, d).start()
    for i in range(len(sources)):
        keep(i).start()
        own_copy(i, req).start()
    for d in range(1, patch_n):
        stale_copy(d, patch).start()

    def relay(number):
        for k in index[number]:
            for d in range(1, chips):
                x_arrival(k, d).wait_recv()
                if chunks[k][3]:
                    for e in range(1, groups):
                        y_copy(k, d, e).start()
                fx_copy(k, d).start()
                if k + AHEAD < len(chunks):
                    x_copy(k + AHEAD, d).start()

    def relay_two(number):
        for k in index[number]:
            if chunks[k][3]:
                for d in range(1, chips):
                    for e in range(1, groups):
                        y_arrival(k, d, e).wait_recv()
                        fy_copy(k, d, e).start()

    def land(number):
        for k in index[number]:
            for d in range(1, chips):
                other_core(k, d, group, fx_send.at[k, d - 1], fx_recv.at[k, d - 1]).wait_recv()
                if chunks[k][3]:
                    for e in range(1, groups):
                        other_core(
                            k, d, group_at(-e),
                            fy_send.at[k, d - 1, e - 1], fy_recv.at[k, d - 1, e - 1],
                        ).wait_recv()

    def own_land(i):
        keep(i).wait()
        own_copy(i, chip * CORES + (1 - core)).wait_recv()

    rows = hidden_ref.shape[0] // 2
    images = 2
    tok = rows // images
    width = hidden_ref.shape[1]
    staged[0].wait()
    staged[1].wait()
    mods = [
        [table_ref[c, pl.ds(step_ref[0, s], 1), :] for c in range(3)] for s in range(2)
    ]
    for s in range(2):
        source = hidden_ref[s * rows : (s + 1) * rows, :].astype(jnp.float32)
        center = source - jnp.mean(source, axis=-1, keepdims=True)
        spread_ = jnp.mean(center * center, axis=-1, keepdims=True)
        normed = center * lax.rsqrt(spread_ + 1e-06)
        mod_s[s * rows : (s + 1) * rows, :] = (
            normed * (1.0 + mods[s][1]) + mods[s][0]
        ).astype(jnp.bfloat16)

    def project(first, last, start, stop):
        n, depth, _ = w_qkv.shape
        return jnp.dot(
            mod_s[first:last, :], w_qkv[:, :, start:stop].reshape(n * depth, stop - start),
            preferred_element_type=jnp.float32,
        ).astype(jnp.bfloat16)

    relay(0)
    relay_two(0)
    own_land(QKV)
    land(0)
    fresh0 = project(0, rows, low, 3 * inner)[:, inner - low :]
    kv0[patch] = fresh0.reshape(images, tok, 2 * inner)
    for d in range(1, patch_n):
        fresh_copy(d, patch).start()
    relay(1)
    fresh1 = project(rows, 2 * rows, low, 3 * inner)[:, inner - low :]
    kv1[patch] = fresh1.reshape(images, tok, 2 * inner)
    next_ref[...] = fresh1
    relay_two(1)
    land(1)
    query_s[...] = project(0, 2 * rows, 0, high)[:, :inner]
    relay(2)

    q_mask = head_mask(inner, 0, jnp.bfloat16)
    v_mask = head_mask(2 * inner - low, inner - low, jnp.float32)

    def self_attend(step, buf):
        for image in range(images):
            first = step * rows + image * tok
            pairs = buf[:, image].reshape(patch_n * tok, 2 * inner)
            result = attend(
                query_s[first : first + tok, :], pairs[:, :inner], pairs[:, low:],
                q_mask, v_mask, None,
            )
            att_s[first : first + tok, :] = result[:, inner - low :].astype(jnp.bfloat16)

    for d in range(1, patch_n):
        stale_copy(d, patch_at(-d)).wait_recv()
    self_attend(0, kv0)
    relay_two(2)
    relay(3)
    relay_two(3)
    relay(4)
    for d in range(1, patch_n):
        fresh_copy(d, patch_at(-d)).wait_recv()
    self_attend(1, kv1)
    relay_two(4)
    own_land(OUT)
    land(2)
    projected = times(att_s[...], w_out)
    parts = []
    for s in range(2):
        span = slice(s * rows, (s + 1) * rows)
        parts.append(
            (hidden_ref[span, :].astype(jnp.float32) + mods[s][2] * projected[span]).astype(
                jnp.bfloat16
            )
        )
    x_one = jnp.concatenate(parts, axis=0)
    own_land(CQ)
    own_land(NEG)
    staged[2].wait()
    land(3)
    cross_query = times(x_one, w_cq).astype(jnp.bfloat16)
    count = len_ref[0]
    n_neg, neg_rows, _ = w_neg.shape
    negative = w_neg[...].reshape(n_neg * neg_rows, 2 * inner)
    for image in range(images):
        pairs = cond_ref[...] if image == 0 else negative
        spans = [slice(s * rows + image * tok, s * rows + (image + 1) * tok) for s in range(2)]
        both = jnp.concatenate([cross_query[span] for span in spans], axis=0)
        result = attend(
            both, pairs[:, :inner], pairs[:, low:], q_mask, v_mask, count if image == 0 else None
        )[:, inner - low :].astype(jnp.bfloat16)
        for s in range(2):
            att_s[spans[s], :] = result[s * tok : (s + 1) * tok]
    own_land(CO)
    land(4)
    added = times(att_s[...], w_co)
    mixed_ref[...] = (x_one.astype(jnp.float32) + added).astype(jnp.bfloat16)

    for k in range(len(chunks)):
        for d in range(1, chips):
            x_copy(k, d).wait_send()
            fx_copy(k, d).wait_send()
            if chunks[k][3]:
                for e in range(1, groups):
                    y_copy(k, d, e).wait_send()
                    fy_copy(k, d, e).wait_send()
    for i in range(len(sources)):
        own_copy(i, req).wait_send()
    for d in range(1, patch_n):
        stale_copy(d, patch).wait_send()
        fresh_copy(d, patch).wait_send()


def solution(mesh):
    groups, patch_n, req_n = mesh.shape["groups"], mesh.shape["patch"], mesh.shape["req"]
    chips = req_n // CORES

    def per_device(
        hidden, stale_kv, cond_kv, uncond_kv, text_len, timestep, mod_table, w_qkv, w_out, w_cq, w_co
    ):
        steps_n, req_here, pair_n, tok, width = hidden.shape
        inner = w_cq.shape[1]
        stages = plan(inner, width, groups)
        count = sum(len(stage) for stage in stages)
        total = steps_n * req_here * pair_n * tok
        vmem = pl.BlockSpec(memory_space=pltpu.VMEM)
        hbm = pl.BlockSpec(memory_space=pltpu.HBM)
        smem = pl.BlockSpec(memory_space=pltpu.SMEM)
        weights = (w_qkv, w_out, w_cq, w_co, uncond_kv)
        dma = pltpu.SemaphoreType.DMA
        table = jnp.transpose(mod_table, (1, 0, 2))
        near = (count, max(chips - 1, 1))
        far = near + (max(groups - 1, 1),)
        line = (max(patch_n - 1, 1),)
        mixed, next_kv = pl.pallas_call(
            functools.partial(kernel, groups, patch_n, req_n, stages),
            out_shape=(
                jax.ShapeDtypeStruct((total, width), jnp.bfloat16),
                jax.ShapeDtypeStruct((pair_n * tok, 2 * inner), jnp.bfloat16),
            ),
            in_specs=[
                smem, smem, hbm, hbm, hbm, hbm, hbm, hbm, hbm, hbm, hbm,
            ],
            out_specs=(vmem, vmem),
            scratch_shapes=[pltpu.VMEM((req_n,) + w.shape, jnp.bfloat16) for w in weights]
            + [
                pltpu.VMEM((patch_n, pair_n, tok, 2 * inner), jnp.bfloat16),
                pltpu.VMEM((patch_n, pair_n, tok, 2 * inner), jnp.bfloat16),
                pltpu.VMEM((total, width), jnp.bfloat16),
                pltpu.VMEM((total, inner), jnp.bfloat16),
                pltpu.VMEM((total, inner), jnp.bfloat16),
                pltpu.VMEM((total, width), jnp.bfloat16),
                pltpu.VMEM(cond_kv.shape[1:], jnp.bfloat16),
                pltpu.VMEM(table.shape, jnp.float32),
                dma((3,)), dma((5,)), dma((5,)), dma((5,)),
                dma(near), dma(near), dma(far), dma(far), dma(near), dma(near), dma(far), dma(far),
                dma(line), dma(line), dma(line), dma(line),
            ],
            compiler_params=pltpu.CompilerParams(
                collective_id=0, has_side_effects=True, vmem_limit_bytes=48 * 1024 * 1024
            ),
        )(
            text_len, timestep,
            *(
                pltpu.with_memory_space_constraint(value, pltpu.HBM)
                for value in (
                    hidden.reshape(total, width), stale_kv.reshape(pair_n, tok, 2 * inner),
                    cond_kv.reshape(cond_kv.shape[1:]), uncond_kv, table,
                    w_qkv, w_out, w_cq, w_co,
                )
            ),
        )
        return mixed.reshape(hidden.shape), next_kv.reshape(stale_kv.shape)

    placed = (
        P(None, ("groups", "req"), None, "patch", None),
        P(("groups", "req"), None, "patch", None),
        P(("groups", "req"), None, None),
        P("req", None),
        P(("groups", "req")),
        P(("groups", "req"), None),
        P(),
        P("req", None),
        P("req", None),
        P("req", None),
        P("req", None),
    )
    return jax.shard_map(
        per_device,
        mesh=mesh,
        in_specs=placed,
        out_specs=(
            P(None, ("groups", "req"), None, "patch", None),
            P(("groups", "req"), None, "patch", None),
        ),
        check_vma=False,
    )
```

```python
import functools
import math

import jax
import jax.numpy as jnp
from jax import lax
from jax.experimental import pallas as pl
from jax.experimental.pallas import tpu as pltpu
from jax.sharding import PartitionSpec as P

HEADS = 8
HDIM = 72
CORES = 2
LANES = 128
PIECE = 256
AHEAD = 6
MESH = pl.DeviceIdType.MESH

QKV, OUT, CQ, CO, NEG = range(5)


def spread(which, start, stop, groups):
    width = (stop - start) // (LANES * groups) * LANES
    chunks = []
    place = start
    while place < start + groups * width:
        piece = min(PIECE, (start + groups * width - place) // groups)
        chunks.append((which, place, piece, True))
        place += groups * piece
    if stop > start + groups * width:
        chunks.append((which, start + groups * width, stop - start - groups * width, False))
    return chunks


def plan(inner, width, groups):
    low = inner // LANES * LANES
    first = spread(QKV, low, 3 * inner, groups)
    stages = [
        first,
        spread(QKV, 0, low, groups),
        spread(OUT, 0, width, groups),
        spread(CQ, 0, inner, groups) + spread(NEG, 0, 2 * inner, groups),
        spread(CO, 0, width, groups),
    ]
    return stages


def times(left, w_ref):
    n, rows, _ = w_ref.shape
    if rows % 16 == 0:
        return jnp.dot(
            left,
            w_ref[...].reshape(n * rows, w_ref.shape[2]),
            preferred_element_type=jnp.float32,
        )
    total = None
    for s in range(n):
        term = jnp.dot(
            left[:, s * rows : (s + 1) * rows], w_ref[s], preferred_element_type=jnp.float32
        )
        total = term if total is None else total + term
    return total


def head_mask(lanes, offset, dtype):
    lane = lax.broadcasted_iota(jnp.int32, (HEADS, 1, lanes), 2) - offset
    first = lax.broadcasted_iota(jnp.int32, (HEADS, 1, lanes), 0) * HDIM
    return jnp.where((lane >= first) & (lane < first + HDIM), 1.0, 0.0).astype(dtype)


def attend(query, keys, values, q_mask, v_mask, count):
    rows, inner = query.shape
    stacked = (query[None] * q_mask).reshape(HEADS * rows, inner)
    scores = lax.dot_general(
        stacked, keys, (((1,), (1,)), ((), ())), preferred_element_type=jnp.float32
    ) * (1.0 / math.sqrt(HDIM))
    if count is not None:
        place = lax.broadcasted_iota(jnp.int32, scores.shape, 1)
        scores = jnp.where(place < count, scores, -1e30)
    expo = jnp.exp(scores - jnp.max(scores, axis=-1, keepdims=True))
    total = jnp.sum(expo, axis=-1, keepdims=True)
    summed = jnp.dot(expo.astype(jnp.bfloat16), values, preferred_element_type=jnp.float32)
    scaled = (summed * (1.0 / total)).reshape(HEADS, rows, values.shape[1])
    return jnp.sum(scaled * v_mask, axis=0)


def kernel(
    groups, patch_n, req_n, stages,
    len_ref, step_ref, hidden_in, stale_ref, cond_in, neg_in, table_in, qkv_in, out_in, cq_in, co_in,
    mixed_ref, next_ref,
    w_qkv, w_out, w_cq, w_co, w_neg, kv0, kv1, mod_s, query_s, att_s,
    hidden_ref, cond_ref, table_ref, in_sem, local_sem, own_send, own_recv, x_send, x_recv, y_send, y_recv, fx_send, fx_recv, fy_send, fy_recv,
    s_send, s_recv, f_send, f_recv,
):
    chips = req_n // CORES
    group = lax.axis_index("groups")
    patch = lax.axis_index("patch")
    req = lax.axis_index("req")
    chip, core = req // CORES, req % CORES
    sibling = (group, patch, chip * CORES + (1 - core))
    sources = (qkv_in, out_in, cq_in, co_in, neg_in)
    bufs = (w_qkv, w_out, w_cq, w_co, w_neg)
    inner = cq_in.shape[1]
    low = inner // LANES * LANES
    high = low + LANES if low < inner else low

    def chip_at(delta):
        return lax.rem(chip + (delta + chips), chips) * CORES + core

    def group_at(delta):
        return lax.rem(group + (delta + groups), groups)

    def patch_at(delta):
        return lax.rem(patch + (delta + patch_n), patch_n)

    staged = [
        pltpu.make_async_copy(src, dst, in_sem.at[i])
        for i, (src, dst) in enumerate(
            ((hidden_in, hidden_ref), (table_in, table_ref), (cond_in, cond_ref))
        )
    ]
    for copy in staged:
        copy.start()
    barrier = pltpu.get_barrier_semaphore()
    friends = [sibling]
    friends += [(group, patch, chip_at(d)) for d in range(1, chips)]
    friends += [(group_at(e), patch, req) for e in range(1, groups)]
    friends += [(group, patch_at(d), req) for d in range(1, patch_n)]
    for friend in friends:
        pl.semaphore_signal(barrier, inc=1, device_id=friend, device_id_type=MESH)
    pl.semaphore_wait(barrier, len(friends))

    chunks = [chunk for stage in stages for chunk in stage]

    def columns(chunk, owner):
        _, start, width, shared = chunk
        if not shared:
            return pl.ds(start, width)
        return pl.ds(pl.multiple_of(start + owner * width, LANES), width)

    def remote(src, dst, send, recv, target):
        return pltpu.make_async_remote_copy(
            src_ref=src, dst_ref=dst, send_sem=send, recv_sem=recv,
            device_id=target, device_id_type=MESH,
        )

    def x_copy(k, d):
        chunk = chunks[k]
        cols = columns(chunk, group)
        return remote(
            sources[chunk[0]].at[:, cols], bufs[chunk[0]].at[req, :, cols],
            x_send.at[k, d - 1], x_recv.at[k, d - 1], (group, patch, chip_at(d)),
        )

    def arrived(k, d, owner, send, recv, target):
        part = bufs[chunks[k][0]].at[chip_at(-d), :, columns(chunks[k], owner)]
        return remote(part, part, send, recv, target)

    def x_arrival(k, d):
        return arrived(k, d, group, x_send.at[k, d - 1], x_recv.at[k, d - 1], sibling)

    def y_copy(k, d, e):
        return arrived(
            k, d, group, y_send.at[k, d - 1, e - 1], y_recv.at[k, d - 1, e - 1],
            (group_at(e), patch, req),
        )

    def y_arrival(k, d, e):
        return arrived(
            k, d, group_at(-e), y_send.at[k, d - 1, e - 1], y_recv.at[k, d - 1, e - 1], sibling
        )

    def fx_copy(k, d):
        return arrived(k, d, group, fx_send.at[k, d - 1], fx_recv.at[k, d - 1], sibling)

    def fy_copy(k, d, e):
        return arrived(
            k, d, group_at(-e), fy_send.at[k, d - 1, e - 1], fy_recv.at[k, d - 1, e - 1], sibling
        )

    def other_core(k, d, owner, send, recv):
        source = lax.rem(chip + (chips - d), chips) * CORES + (1 - core)
        part = bufs[chunks[k][0]].at[source, :, columns(chunks[k], owner)]
        return remote(part, part, send, recv, sibling)

    def own_copy(i, slot):
        return remote(
            sources[i], bufs[i].at[slot], own_send.at[i], own_recv.at[i], sibling
        )

    def keep(i):
        return pltpu.make_async_copy(sources[i], bufs[i].at[req], local_sem.at[i])

    def stale_copy(d, slot):
        return remote(
            stale_ref, kv0.at[slot], s_send.at[d - 1], s_recv.at[d - 1],
            (group, patch_at(d), req),
        )

    def fresh_copy(d, slot):
        return remote(
            kv0.at[patch], kv1.at[slot], f_send.at[d - 1], f_recv.at[d - 1],
            (group, patch_at(d), req),
        )

    index = {}
    place = 0
    for number, stage in enumerate(stages):
        index[number] = list(range(place, place + len(stage)))
        place += len(stage)

    for k in range(min(AHEAD, len(chunks))):
        for d in range(1, chips):
            x_copy(k, d).start()
    for i in range(len(sources)):
        keep(i).start()
        own_copy(i, req).start()
    for d in range(1, patch_n):
        stale_copy(d, patch).start()

    def relay(number):
        for k in index[number]:
            for d in range(1, chips):
                x_arrival(k, d).wait_recv()
                if chunks[k][3]:
                    for e in range(1, groups):
                        y_copy(k, d, e).start()
                fx_copy(k, d).start()
                if k + AHEAD < len(chunks):
                    x_copy(k + AHEAD, d).start()

    def relay_two(number):
        for k in index[number]:
            if chunks[k][3]:
                for d in range(1, chips):
                    for e in range(1, groups):
                        y_arrival(k, d, e).wait_recv()
                        fy_copy(k, d, e).start()

    def land(number):
        for k in index[number]:
            for d in range(1, chips):
                other_core(k, d, group, fx_send.at[k, d - 1], fx_recv.at[k, d - 1]).wait_recv()
                if chunks[k][3]:
                    for e in range(1, groups):
                        other_core(
                            k, d, group_at(-e),
                            fy_send.at[k, d - 1, e - 1], fy_recv.at[k, d - 1, e - 1],
                        ).wait_recv()

    def own_land(i):
        keep(i).wait()
        own_copy(i, chip * CORES + (1 - core)).wait_recv()

    rows = hidden_ref.shape[0] // 2
    images = 2
    tok = rows // images
    width = hidden_ref.shape[1]
    staged[0].wait()
    staged[1].wait()
    mods = [
        [table_ref[c, pl.ds(step_ref[0, s], 1), :] for c in range(3)] for s in range(2)
    ]
    for s in range(2):
        source = hidden_ref[s * rows : (s + 1) * rows, :].astype(jnp.float32)
        center = source - jnp.mean(source, axis=-1, keepdims=True)
        spread_ = jnp.mean(center * center, axis=-1, keepdims=True)
        normed = center * lax.rsqrt(spread_ + 1e-06)
        mod_s[s * rows : (s + 1) * rows, :] = (
            normed * (1.0 + mods[s][1]) + mods[s][0]
        ).astype(jnp.bfloat16)

    def project(first, last, start, stop):
        n, depth, _ = w_qkv.shape
        return jnp.dot(
            mod_s[first:last, :], w_qkv[:, :, start:stop].reshape(n * depth, stop - start),
            preferred_element_type=jnp.float32,
        ).astype(jnp.bfloat16)

    relay(0)
    relay_two(0)
    own_land(QKV)
    land(0)
    fresh0 = project(0, rows, low, 3 * inner)[:, inner - low :]
    kv0[patch] = fresh0.reshape(images, tok, 2 * inner)
    for d in range(1, patch_n):
        fresh_copy(d, patch).start()
    relay(1)
    fresh1 = project(rows, 2 * rows, low, 3 * inner)[:, inner - low :]
    kv1[patch] = fresh1.reshape(images, tok, 2 * inner)
    next_ref[...] = fresh1
    relay_two(1)
    land(1)
    query_s[...] = project(0, 2 * rows, 0, high)[:, :inner]
    relay(2)

    q_mask = head_mask(inner, 0, jnp.bfloat16)
    v_mask = head_mask(2 * inner - low, inner - low, jnp.float32)

    def self_attend(step, buf):
        for image in range(images):
            first = step * rows + image * tok
            pairs = buf[:, image].reshape(patch_n * tok, 2 * inner)
            result = attend(
                query_s[first : first + tok, :], pairs[:, :inner], pairs[:, low:],
                q_mask, v_mask, None,
            )
            att_s[first : first + tok, :] = result[:, inner - low :].astype(jnp.bfloat16)

    for d in range(1, patch_n):
        stale_copy(d, patch_at(-d)).wait_recv()
    self_attend(0, kv0)
    relay_two(2)
    relay(3)
    relay_two(3)
    relay(4)
    for d in range(1, patch_n):
        fresh_copy(d, patch_at(-d)).wait_recv()
    self_attend(1, kv1)
    relay_two(4)
    own_land(OUT)
    land(2)
    projected = times(att_s[...], w_out)
    parts = []
    for s in range(2):
        span = slice(s * rows, (s + 1) * rows)
        parts.append(
            (hidden_ref[span, :].astype(jnp.float32) + mods[s][2] * projected[span]).astype(
                jnp.bfloat16
            )
        )
    x_one = jnp.concatenate(parts, axis=0)
    own_land(CQ)
    own_land(NEG)
    staged[2].wait()
    land(3)
    cross_query = times(x_one, w_cq).astype(jnp.bfloat16)
    count = len_ref[0]
    n_neg, neg_rows, _ = w_neg.shape
    negative = w_neg[...].reshape(n_neg * neg_rows, 2 * inner)
    for image in range(images):
        pairs = cond_ref[...] if image == 0 else negative
        spans = [slice(s * rows + image * tok, s * rows + (image + 1) * tok) for s in range(2)]
        both = jnp.concatenate([cross_query[span] for span in spans], axis=0)
        result = attend(
            both, pairs[:, :inner], pairs[:, low:], q_mask, v_mask, count if image == 0 else None
        )[:, inner - low :].astype(jnp.bfloat16)
        for s in range(2):
            att_s[spans[s], :] = result[s * tok : (s + 1) * tok]
    own_land(CO)
    land(4)
    added = times(att_s[...], w_co)
    mixed_ref[...] = (x_one.astype(jnp.float32) + added).astype(jnp.bfloat16)

    for k in range(len(chunks)):
        for d in range(1, chips):
            x_copy(k, d).wait_send()
            fx_copy(k, d).wait_send()
            if chunks[k][3]:
                for e in range(1, groups):
                    y_copy(k, d, e).wait_send()
                    fy_copy(k, d, e).wait_send()
    for i in range(len(sources)):
        own_copy(i, req).wait_send()
    for d in range(1, patch_n):
        stale_copy(d, patch).wait_send()
        fresh_copy(d, patch).wait_send()


def solution(mesh):
    groups, patch_n, req_n = mesh.shape["groups"], mesh.shape["patch"], mesh.shape["req"]
    chips = req_n // CORES

    def per_device(
        hidden, stale_kv, cond_kv, uncond_kv, text_len, timestep, mod_table, w_qkv, w_out, w_cq, w_co
    ):
        steps_n, req_here, pair_n, tok, width = hidden.shape
        inner = w_cq.shape[1]
        stages = plan(inner, width, groups)
        count = sum(len(stage) for stage in stages)
        total = steps_n * req_here * pair_n * tok
        vmem = pl.BlockSpec(memory_space=pltpu.VMEM)
        hbm = pl.BlockSpec(memory_space=pltpu.HBM)
        smem = pl.BlockSpec(memory_space=pltpu.SMEM)
        weights = (w_qkv, w_out, w_cq, w_co, uncond_kv)
        dma = pltpu.SemaphoreType.DMA
        table = jnp.transpose(mod_table, (1, 0, 2))
        near = (count, max(chips - 1, 1))
        far = near + (max(groups - 1, 1),)
        line = (max(patch_n - 1, 1),)
        mixed, next_kv = pl.pallas_call(
            functools.partial(kernel, groups, patch_n, req_n, stages),
            out_shape=(
                jax.ShapeDtypeStruct((total, width), jnp.bfloat16),
                jax.ShapeDtypeStruct((pair_n * tok, 2 * inner), jnp.bfloat16),
            ),
            in_specs=[
                smem, smem, hbm, hbm, hbm, hbm, hbm, hbm, hbm, hbm, hbm,
            ],
            out_specs=(vmem, vmem),
            scratch_shapes=[pltpu.VMEM((req_n,) + w.shape, jnp.bfloat16) for w in weights]
            + [
                pltpu.VMEM((patch_n, pair_n, tok, 2 * inner), jnp.bfloat16),
                pltpu.VMEM((patch_n, pair_n, tok, 2 * inner), jnp.bfloat16),
                pltpu.VMEM((total, width), jnp.bfloat16),
                pltpu.VMEM((total, inner), jnp.bfloat16),
                pltpu.VMEM((total, inner), jnp.bfloat16),
                pltpu.VMEM((total, width), jnp.bfloat16),
                pltpu.VMEM(cond_kv.shape[1:], jnp.bfloat16),
                pltpu.VMEM(table.shape, jnp.float32),
                dma((3,)), dma((5,)), dma((5,)), dma((5,)),
                dma(near), dma(near), dma(far), dma(far), dma(near), dma(near), dma(far), dma(far),
                dma(line), dma(line), dma(line), dma(line),
            ],
            compiler_params=pltpu.CompilerParams(
                collective_id=0, has_side_effects=True, vmem_limit_bytes=48 * 1024 * 1024
            ),
        )(
            text_len, timestep,
            *(
                pltpu.with_memory_space_constraint(value, pltpu.HBM)
                for value in (
                    hidden.reshape(total, width), stale_kv.reshape(pair_n, tok, 2 * inner),
                    cond_kv.reshape(cond_kv.shape[1:]), uncond_kv, table,
                    w_qkv, w_out, w_cq, w_co,
                )
            ),
        )
        return mixed.reshape(hidden.shape), next_kv.reshape(stale_kv.shape)

    placed = (
        P(None, ("groups", "req"), None, "patch", None),
        P(("groups", "req"), None, "patch", None),
        P(("groups", "req"), None, None),
        P("req", None),
        P(("groups", "req")),
        P(("groups", "req"), None),
        P(),
        P("req", None),
        P("req", None),
        P("req", None),
        P("req", None),
    )
    return jax.shard_map(
        per_device,
        mesh=mesh,
        in_specs=placed,
        out_specs=(
            P(None, ("groups", "req"), None, "patch", None),
            P(("groups", "req"), None, "patch", None),
        ),
        check_vma=False,
    )
```
